32 devices in a mesh: row: 8 (over z, x), col: 4 (over y, core).
Axes of the slice: x: 2, y: 2, z: 4, core: 2. Of those that a mesh axis runs over, the one named last changes fastest.
Arguments:
- innovations: float32 [64, 16384], P(None, ('row', 'col')), may hold values from -300 to 300
- obs_factors: float32 [64, 16384], P(None, ('row', 'col')), may hold values from -6 to 6
- component: int32 [16384], P(('row', 'col')), may hold values 0 or 1
- obs_error: float32 [16384], P(('row', 'col')), may hold values from 0.5 to 2
- coupling: float32 [2, 2], replicated, may hold values from 0.5 to 2
- tile_slots: int32 [8, 4, 8, 3], P('row', 'col'), may hold values from 0 to 7, as said below
Outputs:
- increment: float32 [64, 16384], P(None, ('row', 'col'))
- residual: float32 [64, 16384], P(None, ('row', 'col'))
The draws below stay inside these ranges and needn't reach their ends.
Inputs may be any that keep to these rules, and one draw needn't show every extreme that they name: `tile_slots`: each device's slots name distinct (local block row, local block column) pairs; on some device all 8 slots are live; the live flag is 0 or 1; local block rows are below 4 and local block columns below 8.
All inputs are finite; a program needn't handle non-finite values. No bound on the sum of `component` on one device may be relied on, other than what follows from the above.
Results may differ from the reference program's by a relative error of at most 0.0003.
Values sent between devices are 32-bit elements; how exact they have to be, the bound alone decides.
A program may use at most 64 MiB of HBM per device.

```python
import math
import jax
import jax.numpy as jnp
from jax import lax

TILE = 512
DF = 64
NRHS = 64
ITERS = 3
SLOTS = 8
BLK_DEV = 1
ROW_DEVS = 8
COL_DEVS = 4
NR_LOC = 4
NC_LOC = 8
NOBS = 16384


def factor_field(key):
    factor_key = jax.random.fold_in(key, 7)
    field = jnp.clip(jax.random.normal(factor_key, (DF, NOBS), jnp.float32), -6.0, 6.0)
    return field


def draw_obs_factors(key, part):
    return factor_field(key)


def draw_innovations(key, part):
    first_key = jax.random.fold_in(jax.random.fold_in(key, 3), 0)
    third_key = jax.random.fold_in(jax.random.fold_in(key, 3), 2)
    position = jnp.arange(NOBS, dtype=jnp.float32) / NOBS
    rising = jnp.exp(math.log(3.0) * position)
    loadings = jax.random.normal(third_key, (NRHS, DF), jnp.float32)
    coherent = jnp.dot(loadings, factor_field(key), precision=lax.Precision.HIGHEST) / math.sqrt(DF)
    noise_part = jnp.clip(jax.random.normal(first_key, (NRHS, NOBS), jnp.float32), -6.0, 6.0)
    coherent = jnp.clip(coherent, -6.0, 6.0)
    mixed = 0.5 * noise_part + 0.85 * coherent
    return mixed * rising[None, :]


def draw_tile_slots(key, part):
    first_key, second_key, third_key = jax.random.split(jax.random.fold_in(key, 11), 3)
    devices = ROW_DEVS * COL_DEVS
    cells = NR_LOC * NC_LOC
    scores = jax.random.randint(first_key, (devices, cells), 0, 65536) * cells + jnp.arange(cells, dtype=jnp.int32)[None, :]
    chosen = jnp.argsort(scores, axis=1)[:, :SLOTS].astype(jnp.int32)
    spread = SLOTS - SLOTS // 6
    extra = jax.random.randint(second_key, (devices,), 0, spread + 1)
    counts = SLOTS // 6 + extra * extra // max(spread, 1)
    picked = jax.random.randint(third_key, (), 0, devices)
    counts = jnp.where(jnp.arange(devices, dtype=jnp.int32) == picked, SLOTS, counts)
    live_flags = (jnp.arange(SLOTS, dtype=jnp.int32)[None, :] < counts[:, None]).astype(jnp.int32)
    stacked = jnp.stack([chosen // NC_LOC, chosen % NC_LOC, live_flags], axis=-1)
    return stacked.reshape(ROW_DEVS, COL_DEVS, SLOTS, 3).astype(jnp.int32)


def with_ends(values, own_key, least, high):
    spot = [jax.random.randint(jax.random.fold_in(own_key, axis), (), 0, length) for axis, length in enumerate(values.shape)]
    widest = values.shape.index(max(values.shape))
    beside = spot[:widest] + [(spot[widest] + 1) % values.shape[widest]] + spot[widest + 1:]
    return values.at[tuple(spot)].set(least).at[tuple(beside)].set(high)


def levels(rng, dims, shards, smallest, largest):
    factor_of = 1.0
    for dim, shards_of in shards:
        heights = jax.random.uniform(jax.random.fold_in(jax.random.fold_in(rng, 6), dim), (shards_of,), jnp.float32, smallest / len(shards), largest / len(shards))
        factor_of = factor_of * jnp.repeat(jnp.exp(heights), dims[dim] // shards_of).reshape((-1,) + (1,) * (len(dims) - 1 - dim))
    return factor_of


def setup_inputs(seed: int = 0) -> dict:
    arg_keys = jax.random.split(jax.random.key(seed), 7)
    return {
        "innovations": draw_innovations(jax.random.fold_in(arg_keys[6], 71), 0),
        "obs_factors": draw_obs_factors(jax.random.fold_in(arg_keys[6], 71), 0),
        "component": with_ends((jax.random.randint(arg_keys[2], (NOBS,), 0, 4) < 1).astype(jnp.int32), jax.random.fold_in(arg_keys[2], 1), 0, 1),
        "obs_error": jnp.clip(jnp.exp(math.log(2.0) - 1.3862944 * jax.random.uniform(arg_keys[3], (NOBS,), jnp.float32) ** levels(arg_keys[3], (NOBS,), ((0, 32),), -0.2, 0.2)), 0.5, 2.0),
        "coupling": jnp.clip(jnp.exp(jax.random.uniform(arg_keys[4], (2, 2), jnp.float32, math.log(0.5), math.log(2.0))), 0.5, 2.0),
        "tile_slots": draw_tile_slots(jax.random.fold_in(arg_keys[6], 71), 0),
    }


length_sq = 12.0


def tile_matrix(left_factors, right_factors, left_labels, right_labels, coupling):
    left_norms = jnp.sum(left_factors * left_factors, axis=0)
    right_norms = jnp.sum(right_factors * right_factors, axis=0)
    products = lax.dot_general(left_factors, right_factors, (((0,), (0,)), ((), ())), precision=lax.Precision.HIGHEST, preferred_element_type=jnp.float32)
    pair_coupling = (1.0 - left_labels)[:, None] * ((1.0 - right_labels)[None, :] * coupling[0, 0] + right_labels[None, :] * coupling[0, 1]) + left_labels[:, None] * ((1.0 - right_labels)[None, :] * coupling[1, 0] + right_labels[None, :] * coupling[1, 1])
    return pair_coupling * jnp.exp(-(left_norms[:, None] + right_norms[None, :] - 2.0 * products) / length_sq)


def take_segment(array, block):
    start = (block * TILE).astype(jnp.int32)
    return lax.dynamic_slice_in_dim(array, start, TILE, array.ndim - 1)


def add_segment(vector, block, values):
    start = (block * TILE).astype(jnp.int32)
    last_axis = vector.ndim - 1
    before = lax.dynamic_slice_in_dim(vector, start, TILE, last_axis)
    return lax.dynamic_update_slice_in_dim(vector, before + values, start, last_axis)


def reference(innovations, obs_factors, component, obs_error, coupling, tile_slots):
    labels_float = component.astype(jnp.float32)
    row_devices = jnp.arange(ROW_DEVS, dtype=jnp.int32)[:, None, None]
    column_devices = jnp.arange(COL_DEVS, dtype=jnp.int32)[None, :, None]
    row_block = tile_slots[..., 0]
    column_block = tile_slots[..., 1]
    global_rows = ((row_devices * COL_DEVS + row_block // BLK_DEV) * BLK_DEV + row_block % BLK_DEV).reshape(-1).astype(jnp.int32)
    global_columns = (((column_block // BLK_DEV) * COL_DEVS + column_devices) * BLK_DEV + column_block % BLK_DEV).reshape(-1).astype(jnp.int32)
    live_list = tile_slots[..., 2].reshape(-1).astype(jnp.int32)

    def listed_tile(row_index, column_index):
        return tile_matrix(take_segment(obs_factors, row_index), take_segment(obs_factors, column_index), take_segment(labels_float, row_index), take_segment(labels_float, column_index), coupling)

    def weigh(totals, item):
        row_index, column_index, flag = item

        def work(totals):
            block_matrix = listed_tile(row_index, column_index)
            totals = add_segment(totals, row_index, jnp.sum(block_matrix, axis=1))
            return add_segment(totals, column_index, jnp.sum(block_matrix, axis=0))

        return lax.cond(flag > 0, work, lambda totals: totals, totals), None

    row_weights, unused = lax.scan(weigh, jnp.zeros((NOBS,), jnp.float32), (global_rows, global_columns, live_list))
    diagonal = obs_error + row_weights

    def operate(vector):
        def visit(totals, item):
            row_index, column_index, flag = item

            def work(totals):
                block_matrix = listed_tile(row_index, column_index)
                left_values = take_segment(vector, row_index)
                right_values = take_segment(vector, column_index)
                totals = add_segment(totals, row_index, lax.dot_general(right_values, block_matrix, (((1,), (1,)), ((), ())), precision=lax.Precision.HIGHEST, preferred_element_type=jnp.float32))
                return add_segment(totals, column_index, jnp.dot(left_values, block_matrix, precision=lax.Precision.HIGHEST, preferred_element_type=jnp.float32))

            return lax.cond(flag > 0, work, lambda totals: totals, totals), None

        image, unused = lax.scan(visit, jnp.zeros((NRHS, NOBS), jnp.float32), (global_rows, global_columns, live_list))
        return diagonal[None, :] * vector + image

    increment = jnp.zeros_like(innovations)
    residual = innovations
    direction = innovations
    norm_now = jnp.sum(residual * residual, axis=1)
    for repeat in range(ITERS):
        image = operate(direction)
        alpha = norm_now / jnp.sum(direction * image, axis=1)
        increment = increment + alpha[:, None] * direction
        residual = residual - alpha[:, None] * image
        norm_next = jnp.sum(residual * residual, axis=1)
        direction = residual + (norm_next / norm_now)[:, None] * direction
        norm_now = norm_next
    return increment, residual
```

```python
import functools

import jax
import jax.numpy as jnp
from jax import lax
from jax.experimental import pallas as pl
from jax.experimental.pallas import tpu as pltpu
from jax.sharding import PartitionSpec as P

ITERS = 3
length_sq = 12.0
MESH = pl.DeviceIdType.MESH
VMEM = pl.BlockSpec(memory_space=pltpu.VMEM)
SMEM = pl.BlockSpec(memory_space=pltpu.SMEM)


def peers(rows, cols):
    r, c = lax.axis_index("row"), lax.axis_index("col")
    to_col = [(r, lax.rem(c + k, cols)) for k in range(1, cols)]
    to_row = [(lax.rem(r + k, rows), c) for k in range(1, rows)]
    from_col = [lax.rem(c + cols - k, cols) for k in range(1, cols)]
    from_row = [lax.rem(r + rows - k, rows) for k in range(1, rows)]
    return r, c, to_col, to_row, from_col, from_row


def greet(devices):
    barrier = pltpu.get_barrier_semaphore()
    for device in devices:
        pl.semaphore_signal(barrier, inc=1, device_id=device, device_id_type=MESH)
    pl.semaphore_wait(barrier, len(devices))


def remote(src, dst, send, recv, device):
    return pltpu.make_async_remote_copy(
        src_ref=src, dst_ref=dst, send_sem=send, recv_sem=recv,
        device_id=device, device_id_type=MESH,
    )


def gather_kernel(rows, cols, x, s, by_col, by_row, total, s1, s2, part,
                  send_c, recv_c, send_r, recv_r, send_1, recv_1, send_2, recv_2, own):
    r, c, to_col, to_row, from_col, from_row = peers(rows, cols)
    greet(to_col + to_row)
    small = [remote(s, s1.at[c], send_1.at[k], recv_1.at[k], d) for k, d in enumerate(to_col)]
    for copy in small:
        copy.start()
    bulk = [remote(x, by_row.at[r], send_r.at[k], recv_r.at[k], d) for k, d in enumerate(to_row)]
    bulk += [remote(x, by_col.at[c], send_c.at[k], recv_c.at[k], d) for k, d in enumerate(to_col)]
    for copy in bulk:
        copy.start()
    keep = [
        pltpu.make_async_copy(x, by_col.at[c], own.at[0]),
        pltpu.make_async_copy(x, by_row.at[r], own.at[1]),
        pltpu.make_async_copy(s, s1.at[c], own.at[2]),
    ]
    for copy in keep:
        copy.start()
    keep[2].wait()
    for k, q in enumerate(from_col):
        remote(s, s1.at[q], send_1.at[k], recv_1.at[k], to_col[k]).wait_recv()
    part[...] = jnp.sum(s1[...], axis=0)
    second = [remote(part, s2.at[r], send_2.at[k], recv_2.at[k], d) for k, d in enumerate(to_row)]
    for copy in second:
        copy.start()
    mine = pltpu.make_async_copy(part, s2.at[r], own.at[3])
    mine.start()
    for k, q in enumerate(from_row):
        remote(x, by_row.at[q], send_r.at[k], recv_r.at[k], to_row[k]).wait_recv()
    for k, q in enumerate(from_col):
        remote(x, by_col.at[q], send_c.at[k], recv_c.at[k], to_col[k]).wait_recv()
    for k, q in enumerate(from_row):
        remote(part, s2.at[q], send_2.at[k], recv_2.at[k], to_row[k]).wait_recv()
    mine.wait()
    keep[0].wait()
    keep[1].wait()
    total[...] = jnp.sum(s2[...], axis=0)
    for copy in small + bulk + second:
        copy.wait_send()


def scatter_kernel(rows, cols, by_col, by_row, s, out, total, got_c, got_r, s1, s2, part,
                   send_c, recv_c, send_r, recv_r, send_1, recv_1, send_2, recv_2, own):
    r, c, to_col, to_row, from_col, from_row = peers(rows, cols)
    greet(to_col + to_row)
    small = [remote(s, s1.at[c], send_1.at[k], recv_1.at[k], d) for k, d in enumerate(to_col)]
    for copy in small:
        copy.start()
    bulk = [remote(by_row.at[d[0]], got_r.at[k], send_r.at[k], recv_r.at[k], d)
            for k, d in enumerate(to_row)]
    bulk += [remote(by_col.at[d[1]], got_c.at[k], send_c.at[k], recv_c.at[k], d)
             for k, d in enumerate(to_col)]
    for copy in bulk:
        copy.start()
    keep = pltpu.make_async_copy(s, s1.at[c], own.at[0])
    keep.start()
    keep.wait()
    for k, q in enumerate(from_col):
        remote(s, s1.at[q], send_1.at[k], recv_1.at[k], to_col[k]).wait_recv()
    part[...] = jnp.sum(s1[...], axis=0)
    second = [remote(part, s2.at[r], send_2.at[k], recv_2.at[k], d) for k, d in enumerate(to_row)]
    for copy in second:
        copy.start()
    mine = pltpu.make_async_copy(part, s2.at[r], own.at[1])
    mine.start()
    for copy in bulk:
        copy.wait_recv()
    out[...] = (by_col[c] + by_row[r]) + (jnp.sum(got_c[...], axis=0) + jnp.sum(got_r[...], axis=0))
    for k, q in enumerate(from_row):
        remote(part, s2.at[q], send_2.at[k], recv_2.at[k], to_row[k]).wait_recv()
    mine.wait()
    total[...] = jnp.sum(s2[...], axis=0)
    for copy in small + bulk + second:
        copy.wait_send()


def semaphores(rows, cols):
    counts = [cols - 1, cols - 1, rows - 1, rows - 1, cols - 1, cols - 1, rows - 1, rows - 1, 4]
    return [pltpu.SemaphoreType.DMA((n,)) for n in counts]


def small_scratch(rows, cols):
    return [
        pltpu.VMEM((cols, 8, 128), jnp.float32),
        pltpu.VMEM((rows, 8, 128), jnp.float32),
        pltpu.VMEM((8, 128), jnp.float32),
    ]


def gather(x, s, rows, cols, number):
    f32 = jnp.float32
    return pl.pallas_call(
        functools.partial(gather_kernel, rows, cols),
        out_shape=(
            jax.ShapeDtypeStruct((cols,) + x.shape, f32),
            jax.ShapeDtypeStruct((rows,) + x.shape, f32),
            jax.ShapeDtypeStruct((8, 128), f32),
        ),
        in_specs=[VMEM] * 2,
        out_specs=(VMEM,) * 3,
        scratch_shapes=small_scratch(rows, cols) + semaphores(rows, cols),
        compiler_params=pltpu.CompilerParams(collective_id=number, has_side_effects=True),
    )(x, s)


def scatter(by_col, by_row, s, number):
    f32 = jnp.float32
    cols, rows = by_col.shape[0], by_row.shape[0]
    block = by_col.shape[1:]
    return pl.pallas_call(
        functools.partial(scatter_kernel, rows, cols),
        out_shape=(jax.ShapeDtypeStruct(block, f32), jax.ShapeDtypeStruct((8, 128), f32)),
        in_specs=[VMEM] * 3,
        out_specs=(VMEM,) * 2,
        scratch_shapes=[
            pltpu.VMEM((cols - 1,) + block, f32),
            pltpu.VMEM((rows - 1,) + block, f32),
        ] + small_scratch(rows, cols) + semaphores(rows, cols),
        compiler_params=pltpu.CompilerParams(collective_id=number, has_side_effects=True),
    )(by_col, by_row, s)


def build_kernel(slots, left, left_norm, left_label, right, right_norm, right_label,
                 coupling, high, low):
    number = pl.program_id(0)
    a, b = slots[number, 0], slots[number, 1]

    @pl.when(slots[number, 2] > 0)
    def _():
        products = jnp.dot(
            left[a], right[b], precision=lax.Precision.HIGHEST,
            preferred_element_type=jnp.float32,
        )
        ocean = right_label[b] > 0.5
        first = jnp.where(ocean, coupling[0, 1], coupling[0, 0])
        second = jnp.where(ocean, coupling[1, 1], coupling[1, 0])
        pair = jnp.where(left_label[a] > 0.5, second, first)
        tile = pair * jnp.exp(-(left_norm[a] + right_norm[b] - 2.0 * products) / length_sq)
        top = tile.astype(jnp.bfloat16)
        high[0] = top
        low[0] = (tile - top.astype(jnp.float32)).astype(jnp.bfloat16)


def build(slots, left, left_norm, left_label, right, right_norm, right_label, coupling):
    count, tile = slots.shape[0], left.shape[1]
    stored = jax.ShapeDtypeStruct((count, tile, tile), jnp.bfloat16)
    return pl.pallas_call(
        build_kernel,
        grid=(count,),
        out_shape=(stored, stored),
        in_specs=[SMEM] + [VMEM] * 6 + [SMEM],
        out_specs=(pl.BlockSpec((1, tile, tile), lambda i: (i, 0, 0)),) * 2,
    )(slots, left, left_norm, left_label, right, right_norm, right_label, coupling)


def times(values, high, low, side):
    dims = (((1,), (side,)), ((), ()))
    n = values.shape[0]
    top = values.astype(jnp.bfloat16).astype(jnp.float32)
    both = jnp.concatenate([top, values - top], axis=0).astype(jnp.bfloat16)
    wide = lax.dot_general(both, high, dims, preferred_element_type=jnp.float32)
    rest = lax.dot_general(
        top.astype(jnp.bfloat16), low, dims, preferred_element_type=jnp.float32
    )
    return wide[:n] + (wide[n:] + rest)


def fold(x):
    total = x[:, :128]
    for start in range(128, x.shape[1], 128):
        total = total + x[:, start:start + 128]
    return total


def sweep_kernel(rhs, slots, row_values, column_values, high, low, row_image, column_image, dots):
    number = pl.program_id(0)
    a, b = slots[number, 0], slots[number, 1]
    weigh = row_values.shape[1] > rhs

    @pl.when(number == 0)
    def _():
        row_image[...] = jnp.zeros_like(row_image)
        column_image[...] = jnp.zeros_like(column_image)
        dots[...] = jnp.zeros_like(dots)

    @pl.when(slots[number, 2] > 0)
    def _():
        rv, cv = row_values[a], column_values[b]
        t_high, t_low = high[0], low[0]
        right_part = times(cv, t_high, t_low, 1)
        left_part = times(rv, t_high, t_low, 0)
        row_image[a] += right_part
        column_image[b] += left_part
        rv, cv = rv[:rhs], cv[:rhs]
        amount = 2.0 * fold(right_part[:rhs] * rv)
        if weigh:
            amount = amount + fold(right_part[rhs:rhs + 1] * (rv * rv))
            amount = amount + fold(left_part[rhs:rhs + 1] * (cv * cv))
        dots[...] += amount


def sweep(rhs, slots, row_values, column_values, high, low):
    count, tile = high.shape[0], high.shape[1]
    whole = lambda shape: pl.BlockSpec(shape, lambda i: (0,) * len(shape))
    tiles = pl.BlockSpec((1, tile, tile), lambda i: (i, 0, 0))
    f32 = jnp.float32
    return pl.pallas_call(
        functools.partial(sweep_kernel, rhs),
        grid=(count,),
        out_shape=(
            jax.ShapeDtypeStruct(row_values.shape, f32),
            jax.ShapeDtypeStruct(column_values.shape, f32),
            jax.ShapeDtypeStruct((rhs, 128), f32),
        ),
        in_specs=[SMEM, VMEM, VMEM, tiles, tiles],
        out_specs=(whole(row_values.shape), whole(column_values.shape), whole((rhs, 128))),
    )(slots, row_values, column_values, high, low)


def spread(sums):
    return jnp.pad(sums[None, :], ((0, 7), (0, 128 - sums.shape[0])))


def shards(rows, cols, innovations, obs_factors, component, obs_error, coupling, tile_slots):
    slots = tile_slots[0, 0]
    rhs, tile = innovations.shape
    depth = obs_factors.shape[0]
    labels = jnp.pad(component.astype(jnp.float32)[None, :], ((0, 7), (0, 0)))
    packed = jnp.concatenate([obs_factors, labels, innovations], axis=0)
    by_col, by_row, total = gather(
        packed, spread(jnp.sum(innovations * innovations, axis=1)), rows, cols, 0
    )
    norm_now = total[0, :rhs]

    left = by_col[:, :depth]
    right = by_row[:, :depth]
    high, low = build(
        slots,
        jnp.swapaxes(left, 1, 2),
        jnp.sum(left * left, axis=1)[:, :, None],
        by_col[:, depth][:, :, None],
        right,
        jnp.sum(right * right, axis=1)[:, None, :],
        by_row[:, depth][:, None, :],
        coupling,
    )

    row_values = by_col[:, depth + 8:]
    column_values = by_row[:, depth + 8:]

    def with_ones(values):
        ones = jnp.ones((values.shape[0], 1, tile), jnp.float32)
        rest = jnp.zeros((values.shape[0], 15, tile), jnp.float32)
        return jnp.concatenate([values, ones, rest], axis=1)

    increment = jnp.zeros_like(innovations)
    residual = innovations
    direction = innovations
    diagonal = None
    for repeat in range(ITERS):
        if repeat == 0:
            row_image, column_image, dots = sweep(
                rhs, slots, with_ones(row_values), with_ones(column_values), high, low
            )
            row_image, column_image = row_image[:, :rhs + 8], column_image[:, :rhs + 8]
            own = obs_error
        else:
            row_image, column_image, dots = sweep(
                rhs, slots, row_values, column_values, high, low
            )
            own = diagonal
        part = jnp.sum(dots, axis=1) + jnp.sum(own[None, :] * direction * direction, axis=1)
        product, total = scatter(row_image, column_image, spread(part), 1 if repeat == 0 else 2)
        if repeat == 0:
            diagonal = obs_error + product[rhs]
        image = diagonal[None, :] * direction + product[:rhs]
        alpha = norm_now / total[0, :rhs]
        increment = increment + alpha[:, None] * direction
        residual = residual - alpha[:, None] * image
        if repeat + 1 < ITERS:
            by_col, by_row, total = gather(
                residual, spread(jnp.sum(residual * residual, axis=1)), rows, cols, 3
            )
            norm_next = total[0, :rhs]
            beta = (norm_next / norm_now)[:, None]
            direction = residual + beta * direction
            row_values = by_col + beta * row_values
            column_values = by_row + beta * column_values
            norm_now = norm_next
    return (increment, residual)


def solution(mesh):
    return jax.shard_map(
        functools.partial(shards, mesh.shape["row"], mesh.shape["col"]),
        mesh=mesh,
        in_specs=(
            P(None, ("row", "col")),
            P(None, ("row", "col")),
            P(("row", "col")),
            P(("row", "col")),
            P(),
            P("row", "col", None, None),
        ),
        out_specs=(P(None, ("row", "col")), P(None, ("row", "col"))),
        check_vma=False,
    )
```

```python
import functools

import jax
import jax.numpy as jnp
from jax import lax
from jax.experimental import pallas as pl
from jax.experimental.pallas import tpu as pltpu
from jax.sharding import PartitionSpec as P

ITERS = 3
length_sq = 12.0
MESH = pl.DeviceIdType.MESH
VMEM = pl.BlockSpec(memory_space=pltpu.VMEM)
SMEM = pl.BlockSpec(memory_space=pltpu.SMEM)


def peers(rows, cols):
    r, c = lax.axis_index("row"), lax.axis_index("col")
    to_col = [(r, lax.rem(c + k, cols)) for k in range(1, cols)]
    to_row = [(lax.rem(r + k, rows), c) for k in range(1, rows)]
    from_col = [lax.rem(c + cols - k, cols) for k in range(1, cols)]
    from_row = [lax.rem(r + rows - k, rows) for k in range(1, rows)]
    return r, c, to_col, to_row, from_col, from_row


def greet(devices):
    barrier = pltpu.get_barrier_semaphore()
    for device in devices:
        pl.semaphore_signal(barrier, inc=1, device_id=device, device_id_type=MESH)
    pl.semaphore_wait(barrier, len(devices))


def remote(src, dst, send, recv, device):
    return pltpu.make_async_remote_copy(
        src_ref=src, dst_ref=dst, send_sem=send, recv_sem=recv,
        device_id=device, device_id_type=MESH,
    )


def legs(rows):
    outer = 4 if rows % 4 == 0 else rows
    order = sorted(range(1, outer), key=lambda k: (abs(2 * k - outer), k))
    return outer, rows // outer, order


def gather_kernel(rows, cols, x, s, by_col, by_row, total, s1, s2, part,
                  send_c, recv_c, send_z, recv_z, send_x, recv_x,
                  send_1, recv_1, send_2, recv_2, own):
    r, c, to_col, to_row, from_col, from_row = peers(rows, cols)
    outer, inner, order = legs(rows)
    z, w = lax.div(r, inner), lax.rem(r, inner)
    greet(to_col + to_row)
    small = [remote(s, s1.at[c], send_1.at[k], recv_1.at[k], d) for k, d in enumerate(to_col)]
    for copy in small:
        copy.start()
    to_z = {k: (lax.rem(z + k, outer) * inner + w, c) for k in order}
    to_x = {j: (z * inner + lax.rem(w + j, inner), c) for j in range(1, inner)}
    from_z = {k: lax.rem(z + outer - k, outer) for k in [0] + order}
    from_x = {j: lax.rem(w + inner - j, inner) for j in range(1, inner)}

    def along(k, slot):
        return remote(x, by_row.at[slot], send_z.at[k - 1], recv_z.at[k - 1], to_z[k])

    def across(k, j, slot):
        source = x if k == 0 else by_row.at[slot]
        return remote(source, by_row.at[slot], send_x.at[k, j - 1], recv_x.at[k, j - 1], to_x[j])

    bulk = [along(k, r) for k in order]
    bulk += [across(0, j, r) for j in to_x]
    bulk += [remote(x, by_col.at[c], send_c.at[k], recv_c.at[k], d) for k, d in enumerate(to_col)]
    for copy in bulk:
        copy.start()
    keep = [
        pltpu.make_async_copy(x, by_col.at[c], own.at[0]),
        pltpu.make_async_copy(x, by_row.at[r], own.at[1]),
        pltpu.make_async_copy(s, s1.at[c], own.at[2]),
    ]
    for copy in keep:
        copy.start()
    keep[2].wait()
    for k, q in enumerate(from_col):
        remote(s, s1.at[q], send_1.at[k], recv_1.at[k], to_col[k]).wait_recv()
    part[...] = jnp.sum(s1[...], axis=0)
    second = [remote(part, s2.at[r], send_2.at[k], recv_2.at[k], d) for k, d in enumerate(to_row)]
    for copy in second:
        copy.start()
    mine = pltpu.make_async_copy(part, s2.at[r], own.at[3])
    mine.start()
    for k in order:
        slot = from_z[k] * inner + w
        along(k, slot).wait_recv()
        for j in to_x:
            copy = across(k, j, slot)
            copy.start()
            bulk.append(copy)
    for k, q in enumerate(from_col):
        remote(x, by_col.at[q], send_c.at[k], recv_c.at[k], to_col[k]).wait_recv()
    for k in [0] + order:
        for j in to_x:
            across(k, j, from_z[k] * inner + from_x[j]).wait_recv()
    for k, q in enumerate(from_row):
        remote(part, s2.at[q], send_2.at[k], recv_2.at[k], to_row[k]).wait_recv()
    mine.wait()
    keep[0].wait()
    keep[1].wait()
    total[...] = jnp.sum(s2[...], axis=0)
    for copy in small + bulk + second:
        copy.wait_send()


def scatter_kernel(rows, cols, by_col, by_row, s, out, total, got_c, got_z, got_x, stage,
                   s1, s2, part, send_c, recv_c, send_z, recv_z, send_x, recv_x,
                   send_1, recv_1, send_2, recv_2, own):
    r, c, to_col, to_row, from_col, from_row = peers(rows, cols)
    outer, inner, order = legs(rows)
    z, w = lax.div(r, inner), lax.rem(r, inner)
    greet(to_col + to_row)
    small = [remote(s, s1.at[c], send_1.at[k], recv_1.at[k], d) for k, d in enumerate(to_col)]
    for copy in small:
        copy.start()
    across = {}
    for k in order + [0]:
        for j in range(1, inner):
            side = lax.rem(w + j, inner)
            across[k, j] = remote(
                by_row.at[lax.rem(z + k, outer) * inner + side], got_x.at[k, j - 1],
                send_x.at[k, j - 1], recv_x.at[k, j - 1], (z * inner + side, c),
            )
            across[k, j].start()
    flat = [remote(by_col.at[d[1]], got_c.at[k], send_c.at[k], recv_c.at[k], d)
            for k, d in enumerate(to_col)]
    for copy in flat:
        copy.start()
    keep = pltpu.make_async_copy(s, s1.at[c], own.at[0])
    keep.start()
    keep.wait()
    for k, q in enumerate(from_col):
        remote(s, s1.at[q], send_1.at[k], recv_1.at[k], to_col[k]).wait_recv()
    part[...] = jnp.sum(s1[...], axis=0)
    second = [remote(part, s2.at[r], send_2.at[k], recv_2.at[k], d) for k, d in enumerate(to_row)]
    for copy in second:
        copy.start()
    mine = pltpu.make_async_copy(part, s2.at[r], own.at[1])
    mine.start()

    def joined(k):
        value = by_row[lax.rem(z + k, outer) * inner + w]
        for j in range(1, inner):
            across[k, j].wait_recv()
            value = value + got_x[k, j - 1]
        return value

    along = []
    for k in order:
        stage[k - 1] = joined(k)
        copy = remote(stage.at[k - 1], got_z.at[k - 1], send_z.at[k - 1], recv_z.at[k - 1],
                      (lax.rem(z + k, outer) * inner + w, c))
        copy.start()
        along.append(copy)
    for copy in flat:
        copy.wait_recv()
    out[...] = joined(0) + (by_col[c] + jnp.sum(got_c[...], axis=0))
    for copy in along:
        copy.wait_recv()
    out[...] += jnp.sum(got_z[...], axis=0)
    for k, q in enumerate(from_row):
        remote(part, s2.at[q], send_2.at[k], recv_2.at[k], to_row[k]).wait_recv()
    mine.wait()
    total[...] = jnp.sum(s2[...], axis=0)
    for copy in small + flat + along + second + list(across.values()):
        copy.wait_send()


def semaphores(rows, cols):
    outer, inner, order = legs(rows)
    sides = (outer, max(inner - 1, 1))
    shapes = [(cols - 1,)] * 2 + [(outer - 1,)] * 2 + [sides] * 2
    shapes += [(cols - 1,)] * 2 + [(rows - 1,)] * 2 + [(4,)]
    return [pltpu.SemaphoreType.DMA(shape) for shape in shapes]


def small_scratch(rows, cols):
    return [
        pltpu.VMEM((cols, 8, 128), jnp.float32),
        pltpu.VMEM((rows, 8, 128), jnp.float32),
        pltpu.VMEM((8, 128), jnp.float32),
    ]


def gather(x, s, rows, cols, number):
    f32 = jnp.float32
    return pl.pallas_call(
        functools.partial(gather_kernel, rows, cols),
        out_shape=(
            jax.ShapeDtypeStruct((cols,) + x.shape, f32),
            jax.ShapeDtypeStruct((rows,) + x.shape, f32),
            jax.ShapeDtypeStruct((8, 128), f32),
        ),
        in_specs=[VMEM] * 2,
        out_specs=(VMEM,) * 3,
        scratch_shapes=small_scratch(rows, cols) + semaphores(rows, cols),
        compiler_params=pltpu.CompilerParams(collective_id=number, has_side_effects=True),
    )(x, s)


def scatter(by_col, by_row, s, number):
    f32 = jnp.float32
    cols, rows = by_col.shape[0], by_row.shape[0]
    block = by_col.shape[1:]
    outer, inner, order = legs(rows)
    return pl.pallas_call(
        functools.partial(scatter_kernel, rows, cols),
        out_shape=(jax.ShapeDtypeStruct(block, f32), jax.ShapeDtypeStruct((8, 128), f32)),
        in_specs=[VMEM] * 3,
        out_specs=(VMEM,) * 2,
        scratch_shapes=[
            pltpu.VMEM((cols - 1,) + block, f32),
            pltpu.VMEM((outer - 1,) + block, f32),
            pltpu.VMEM((outer, max(inner - 1, 1)) + block, f32),
            pltpu.VMEM((outer - 1,) + block, f32),
        ] + small_scratch(rows, cols) + semaphores(rows, cols),
        compiler_params=pltpu.CompilerParams(collective_id=number, has_side_effects=True),
    )(by_col, by_row, s)


def build_kernel(depth, slots, by_col, by_row, coupling, high, low):
    number = pl.program_id(0)
    a, b = slots[number, 0], slots[number, 1]

    @pl.when(slots[number, 2] > 0)
    def _():
        left = jnp.transpose(by_col[a, :depth + 8])
        left, left_label = left[:, :depth], left[:, depth:depth + 1]
        right, right_label = by_row[b, :depth], by_row[b, depth:depth + 1]
        left_norm = jnp.sum(left * left, axis=1, keepdims=True)
        right_norm = jnp.sum(right * right, axis=0, keepdims=True)
        products = jnp.dot(
            left, right, precision=lax.Precision.HIGHEST, preferred_element_type=jnp.float32
        )
        ocean = right_label > 0.5
        first = jnp.where(ocean, coupling[0, 1], coupling[0, 0])
        second = jnp.where(ocean, coupling[1, 1], coupling[1, 0])
        pair = jnp.where(left_label > 0.5, second, first)
        tile = pair * jnp.exp(-(left_norm + right_norm - 2.0 * products) / length_sq)
        top = tile.astype(jnp.bfloat16)
        high[0] = top
        low[0] = (tile - top.astype(jnp.float32)).astype(jnp.bfloat16)


def build(depth, slots, by_col, by_row, coupling):
    count, tile = slots.shape[0], by_col.shape[2]
    stored = jax.ShapeDtypeStruct((count, tile, tile), jnp.bfloat16)
    return pl.pallas_call(
        functools.partial(build_kernel, depth),
        grid=(count,),
        out_shape=(stored, stored),
        in_specs=[SMEM, VMEM, VMEM, SMEM],
        out_specs=(pl.BlockSpec((1, tile, tile), lambda i: (i, 0, 0)),) * 2,
    )(slots, by_col, by_row, coupling)


def times(values, high, low, side):
    dims = (((1,), (side,)), ((), ()))
    n = values.shape[0]
    top = values.astype(jnp.bfloat16).astype(jnp.float32)
    both = jnp.concatenate([top, values - top], axis=0).astype(jnp.bfloat16)
    wide = lax.dot_general(both, high, dims, preferred_element_type=jnp.float32)
    rest = lax.dot_general(
        top.astype(jnp.bfloat16), low, dims, preferred_element_type=jnp.float32
    )
    return wide[:n] + (wide[n:] + rest)


def fold(x):
    total = x[:, :128]
    for start in range(128, x.shape[1], 128):
        total = total + x[:, start:start + 128]
    return total


def sweep_kernel(rhs, start, slots, row_values, column_values, high, low,
                 row_image, column_image, dots):
    number = pl.program_id(0)
    a, b = slots[number, 0], slots[number, 1]
    kept = row_image.shape[1]
    weigh = kept > rhs

    @pl.when(number == 0)
    def _():
        row_image[...] = jnp.zeros_like(row_image)
        column_image[...] = jnp.zeros_like(column_image)
        dots[...] = jnp.zeros_like(dots)

    @pl.when(slots[number, 2] > 0)
    def _():
        rv, cv = row_values[a, start:start + rhs], column_values[b, start:start + rhs]
        t_high, t_low = high[0], low[0]
        rows, columns = rv, cv
        if weigh:
            ones = jnp.ones((16, rv.shape[1]), jnp.float32)
            rows = jnp.concatenate([rv, ones], axis=0)
            columns = jnp.concatenate([cv, ones], axis=0)
        right_part = times(columns, t_high, t_low, 1)
        left_part = times(rows, t_high, t_low, 0)
        row_image[a] += right_part[:kept]
        column_image[b] += left_part[:kept]
        amount = 2.0 * fold(right_part[:rhs] * rv)
        if weigh:
            amount = amount + fold(right_part[rhs:rhs + 1] * (rv * rv))
            amount = amount + fold(left_part[rhs:rhs + 1] * (cv * cv))
        dots[...] += amount


def sweep(rhs, start, kept, slots, row_values, column_values, high, low):
    count, tile = high.shape[0], high.shape[1]
    whole = lambda shape: pl.BlockSpec(shape, lambda i: (0,) * len(shape))
    tiles = pl.BlockSpec((1, tile, tile), lambda i: (i, 0, 0))
    shapes = (
        (row_values.shape[0], kept, tile), (column_values.shape[0], kept, tile), (rhs, 128)
    )
    return pl.pallas_call(
        functools.partial(sweep_kernel, rhs, start),
        grid=(count,),
        out_shape=tuple(jax.ShapeDtypeStruct(shape, jnp.float32) for shape in shapes),
        in_specs=[SMEM, VMEM, VMEM, tiles, tiles],
        out_specs=tuple(whole(shape) for shape in shapes),
    )(slots, row_values, column_values, high, low)


def spread(sums):
    return jnp.pad(sums[None, :], ((0, 7), (0, 128 - sums.shape[0])))


def shards(rows, cols, innovations, obs_factors, component, obs_error, coupling, tile_slots):
    slots = tile_slots[0, 0]
    rhs = innovations.shape[0]
    depth = obs_factors.shape[0]
    labels = jnp.pad(component.astype(jnp.float32)[None, :], ((0, 7), (0, 0)))
    packed = jnp.concatenate([obs_factors, labels, innovations], axis=0)
    by_col, by_row, total = gather(
        packed, spread(jnp.sum(innovations * innovations, axis=1)), rows, cols, 0
    )
    norm_now = total[0, :rhs]

    high, low = build(depth, slots, by_col, by_row, coupling)
    row_values = by_col[:, depth + 8:]
    column_values = by_row[:, depth + 8:]

    increment = jnp.zeros_like(innovations)
    residual = innovations
    direction = innovations
    diagonal = None
    for repeat in range(ITERS):
        if repeat == 0:
            row_image, column_image, dots = sweep(
                rhs, depth + 8, rhs + 8, slots, by_col, by_row, high, low
            )
            own = obs_error
        else:
            row_image, column_image, dots = sweep(
                rhs, 0, rhs, slots, row_values, column_values, high, low
            )
            own = diagonal
        part = jnp.sum(dots, axis=1) + jnp.sum(own[None, :] * direction * direction, axis=1)
        product, total = scatter(row_image, column_image, spread(part), 1 if repeat == 0 else 2)
        if repeat == 0:
            diagonal = obs_error + product[rhs]
        image = diagonal[None, :] * direction + product[:rhs]
        alpha = norm_now / total[0, :rhs]
        increment = increment + alpha[:, None] * direction
        residual = residual - alpha[:, None] * image
        if repeat + 1 < ITERS:
            by_col, by_row, total = gather(
                residual, spread(jnp.sum(residual * residual, axis=1)), rows, cols, 3
            )
            norm_next = total[0, :rhs]
            beta = (norm_next / norm_now)[:, None]
            direction = residual + beta * direction
            row_values = by_col + beta * row_values
            column_values = by_row + beta * column_values
            norm_now = norm_next
    return (increment, residual)


def solution(mesh):
    return jax.shard_map(
        functools.partial(shards, mesh.shape["row"], mesh.shape["col"]),
        mesh=mesh,
        in_specs=(
            P(None, ("row", "col")),
            P(None, ("row", "col")),
            P(("row", "col")),
            P(("row", "col")),
            P(),
            P("row", "col", None, None),
        ),
        out_specs=(P(None, ("row", "col")), P(None, ("row", "col"))),
        check_vma=False,
    )
```

```python
import functools

import jax
import jax.numpy as jnp
from jax import lax
from jax.experimental import pallas as pl
from jax.experimental.pallas import tpu as pltpu
from jax.sharding import PartitionSpec as P

ITERS = 3
length_sq = 12.0
MESH = pl.DeviceIdType.MESH
VMEM = pl.BlockSpec(memory_space=pltpu.VMEM)
SMEM = pl.BlockSpec(memory_space=pltpu.SMEM)


def peers(rows, cols):
    r, c = lax.axis_index("row"), lax.axis_index("col")
    to_col = [(r, lax.rem(c + k, cols)) for k in range(1, cols)]
    to_row = [(lax.rem(r + k, rows), c) for k in range(1, rows)]
    from_col = [lax.rem(c + cols - k, cols) for k in range(1, cols)]
    from_row = [lax.rem(r + rows - k, rows) for k in range(1, rows)]
    return r, c, to_col, to_row, from_col, from_row


def greet(devices):
    barrier = pltpu.get_barrier_semaphore()
    for device in devices:
        pl.semaphore_signal(barrier, inc=1, device_id=device, device_id_type=MESH)
    pl.semaphore_wait(barrier, len(devices))


def remote(src, dst, send, recv, device):
    return pltpu.make_async_remote_copy(
        src_ref=src, dst_ref=dst, send_sem=send, recv_sem=recv,
        device_id=device, device_id_type=MESH,
    )


def legs(rows):
    outer = 4 if rows % 4 == 0 else rows
    order = sorted(range(1, outer), key=lambda k: (abs(2 * k - outer), k))
    return outer, rows // outer, order


def gather_kernel(rows, cols, x, s, by_col, by_row, total, s1, s2, part,
                  send_c, recv_c, send_z, recv_z, send_x, recv_x,
                  send_1, recv_1, send_2, recv_2, own):
    r, c, to_col, to_row, from_col, from_row = peers(rows, cols)
    outer, inner, order = legs(rows)
    z, w = lax.div(r, inner), lax.rem(r, inner)
    greet(to_col + to_row)
    small = [remote(s, s1.at[c], send_1.at[k], recv_1.at[k], d) for k, d in enumerate(to_col)]
    for copy in small:
        copy.start()
    to_z = {k: (lax.rem(z + k, outer) * inner + w, c) for k in order}
    to_x = {j: (z * inner + lax.rem(w + j, inner), c) for j in range(1, inner)}
    from_z = {k: lax.rem(z + outer - k, outer) for k in [0] + order}
    from_x = {j: lax.rem(w + inner - j, inner) for j in range(1, inner)}

    def along(k, slot):
        return remote(x, by_row.at[slot], send_z.at[k - 1], recv_z.at[k - 1], to_z[k])

    def across(k, j, slot):
        source = x if k == 0 else by_row.at[slot]
        return remote(source, by_row.at[slot], send_x.at[k, j - 1], recv_x.at[k, j - 1], to_x[j])

    bulk = [along(k, r) for k in order]
    bulk += [across(0, j, r) for j in to_x]
    bulk += [remote(x, by_col.at[c], send_c.at[k], recv_c.at[k], d) for k, d in enumerate(to_col)]
    for copy in bulk:
        copy.start()
    keep = [
        pltpu.make_async_copy(x, by_col.at[c], own.at[0]),
        pltpu.make_async_copy(x, by_row.at[r], own.at[1]),
        pltpu.make_async_copy(s, s1.at[c], own.at[2]),
    ]
    for copy in keep:
        copy.start()
    keep[2].wait()
    for k, q in enumerate(from_col):
        remote(s, s1.at[q], send_1.at[k], recv_1.at[k], to_col[k]).wait_recv()
    part[...] = jnp.sum(s1[...], axis=0)
    second = [remote(part, s2.at[r], send_2.at[k], recv_2.at[k], d) for k, d in enumerate(to_row)]
    for copy in second:
        copy.start()
    mine = pltpu.make_async_copy(part, s2.at[r], own.at[3])
    mine.start()
    for k in order:
        slot = from_z[k] * inner + w
        along(k, slot).wait_recv()
        for j in to_x:
            copy = across(k, j, slot)
            copy.start()
            bulk.append(copy)
    for k, q in enumerate(from_col):
        remote(x, by_col.at[q], send_c.at[k], recv_c.at[k], to_col[k]).wait_recv()
    for k in [0] + order:
        for j in to_x:
            across(k, j, from_z[k] * inner + from_x[j]).wait_recv()
    for k, q in enumerate(from_row):
        remote(part, s2.at[q], send_2.at[k], recv_2.at[k], to_row[k]).wait_recv()
    mine.wait()
    keep[0].wait()
    keep[1].wait()
    total[...] = jnp.sum(s2[...], axis=0)
    for copy in small + bulk + second:
        copy.wait_send()


def scatter_kernel(rows, cols, by_col, by_row, s, out, total, got_c, got_z, got_x, stage,
                   s1, s2, part, send_c, recv_c, send_z, recv_z, send_x, recv_x,
                   send_1, recv_1, send_2, recv_2, own):
    r, c, to_col, to_row, from_col, from_row = peers(rows, cols)
    outer, inner, order = legs(rows)
    z, w = lax.div(r, inner), lax.rem(r, inner)
    greet(to_col + to_row)
    small = [remote(s, s1.at[c], send_1.at[k], recv_1.at[k], d) for k, d in enumerate(to_col)]
    for copy in small:
        copy.start()
    across = {}
    for k in order + [0]:
        for j in range(1, inner):
            side = lax.rem(w + j, inner)
            across[k, j] = remote(
                by_row.at[lax.rem(z + k, outer) * inner + side], got_x.at[k, j - 1],
                send_x.at[k, j - 1], recv_x.at[k, j - 1], (z * inner + side, c),
            )
            across[k, j].start()
    flat = [remote(by_col.at[d[1]], got_c.at[k], send_c.at[k], recv_c.at[k], d)
            for k, d in enumerate(to_col)]
    for copy in flat:
        copy.start()
    keep = pltpu.make_async_copy(s, s1.at[c], own.at[0])
    keep.start()
    keep.wait()
    for k, q in enumerate(from_col):
        remote(s, s1.at[q], send_1.at[k], recv_1.at[k], to_col[k]).wait_recv()
    part[...] = jnp.sum(s1[...], axis=0)
    second = [remote(part, s2.at[r], send_2.at[k], recv_2.at[k], d) for k, d in enumerate(to_row)]
    for copy in second:
        copy.start()
    mine = pltpu.make_async_copy(part, s2.at[r], own.at[1])
    mine.start()

    def joined(k):
        value = by_row[lax.rem(z + k, outer) * inner + w]
        for j in range(1, inner):
            across[k, j].wait_recv()
            value = value + got_x[k, j - 1]
        return value

    along = []
    for k in order:
        stage[k - 1] = joined(k)
        copy = remote(stage.at[k - 1], got_z.at[k - 1], send_z.at[k - 1], recv_z.at[k - 1],
                      (lax.rem(z + k, outer) * inner + w, c))
        copy.start()
        along.append(copy)
    for copy in flat:
        copy.wait_recv()
    out[...] = joined(0) + (by_col[c] + jnp.sum(got_c[...], axis=0))
    for copy in along:
        copy.wait_recv()
    out[...] += jnp.sum(got_z[...], axis=0)
    for k, q in enumerate(from_row):
        remote(part, s2.at[q], send_2.at[k], recv_2.at[k], to_row[k]).wait_recv()
    mine.wait()
    total[...] = jnp.sum(s2[...], axis=0)
    for copy in small + flat + along + second + list(across.values()):
        copy.wait_send()


def semaphores(rows, cols):
    outer, inner, order = legs(rows)
    sides = (outer, max(inner - 1, 1))
    shapes = [(cols - 1,)] * 2 + [(outer - 1,)] * 2 + [sides] * 2
    shapes += [(cols - 1,)] * 2 + [(rows - 1,)] * 2 + [(4,)]
    return [pltpu.SemaphoreType.DMA(shape) for shape in shapes]


def small_scratch(rows, cols):
    return [
        pltpu.VMEM((cols, 8, 128), jnp.float32),
        pltpu.VMEM((rows, 8, 128), jnp.float32),
        pltpu.VMEM((8, 128), jnp.float32),
    ]


def gather(x, s, rows, cols, number):
    f32 = jnp.float32
    return pl.pallas_call(
        functools.partial(gather_kernel, rows, cols),
        out_shape=(
            jax.ShapeDtypeStruct((cols,) + x.shape, f32),
            jax.ShapeDtypeStruct((rows,) + x.shape, f32),
            jax.ShapeDtypeStruct((8, 128), f32),
        ),
        in_specs=[VMEM] * 2,
        out_specs=(VMEM,) * 3,
        scratch_shapes=small_scratch(rows, cols) + semaphores(rows, cols),
        compiler_params=pltpu.CompilerParams(collective_id=number, has_side_effects=True),
    )(x, s)


def scatter(by_col, by_row, s, number):
    f32 = jnp.float32
    cols, rows = by_col.shape[0], by_row.shape[0]
    block = by_col.shape[1:]
    outer, inner, order = legs(rows)
    return pl.pallas_call(
        functools.partial(scatter_kernel, rows, cols),
        out_shape=(jax.ShapeDtypeStruct(block, f32), jax.ShapeDtypeStruct((8, 128), f32)),
        in_specs=[VMEM] * 3,
        out_specs=(VMEM,) * 2,
        scratch_shapes=[
            pltpu.VMEM((cols - 1,) + block, f32),
            pltpu.VMEM((outer - 1,) + block, f32),
            pltpu.VMEM((outer, max(inner - 1, 1)) + block, f32),
            pltpu.VMEM((outer - 1,) + block, f32),
        ] + small_scratch(rows, cols) + semaphores(rows, cols),
        compiler_params=pltpu.CompilerParams(collective_id=number, has_side_effects=True),
    )(by_col, by_row, s)


def build_kernel(depth, slots, by_col, by_row, coupling, high, low):
    number = pl.program_id(0)
    a, b = slots[number, 0], slots[number, 1]

    @pl.when(slots[number, 2] > 0)
    def _():
        left = jnp.transpose(by_col[a, :depth + 8])
        left, left_label = left[:, :depth], left[:, depth:depth + 1]
        right, right_label = by_row[b, :depth], by_row[b, depth:depth + 1]
        left_norm = jnp.sum(left * left, axis=1, keepdims=True)
        right_norm = jnp.sum(right * right, axis=0, keepdims=True)
        products = jnp.dot(
            left, right, precision=lax.Precision.HIGHEST, preferred_element_type=jnp.float32
        )
        ocean = right_label > 0.5
        first = jnp.where(ocean, coupling[0, 1], coupling[0, 0])
        second = jnp.where(ocean, coupling[1, 1], coupling[1, 0])
        pair = jnp.where(left_label > 0.5, second, first)
        tile = pair * jnp.exp(-(left_norm + right_norm - 2.0 * products) / length_sq)
        top = tile.astype(jnp.bfloat16)
        high[0] = top
        low[0] = (tile - top.astype(jnp.float32)).astype(jnp.bfloat16)


def build(depth, slots, by_col, by_row, coupling):
    count, tile = slots.shape[0], by_col.shape[2]
    stored = jax.ShapeDtypeStruct((count, tile, tile), jnp.bfloat16)
    return pl.pallas_call(
        functools.partial(build_kernel, depth),
        grid=(count,),
        out_shape=(stored, stored),
        in_specs=[SMEM, VMEM, VMEM, SMEM],
        out_specs=(pl.BlockSpec((1, tile, tile), lambda i: (i, 0, 0)),) * 2,
    )(slots, by_col, by_row, coupling)


def times(values, high, low, side):
    dims = (((1,), (side,)), ((), ()))
    n = values.shape[0]
    top = values.astype(jnp.bfloat16).astype(jnp.float32)
    both = jnp.concatenate([top, values - top], axis=0).astype(jnp.bfloat16)
    wide = lax.dot_general(both, high, dims, preferred_element_type=jnp.float32)
    rest = lax.dot_general(
        top.astype(jnp.bfloat16), low, dims, preferred_element_type=jnp.float32
    )
    return wide[:n] + (wide[n:] + rest)


def fold(x):
    total = x[:, :128]
    for start in range(128, x.shape[1], 128):
        total = total + x[:, start:start + 128]
    return total


def sweep_kernel(rhs, start, slots, row_values, column_values, high, low,
                 row_image, column_image, dots):
    number = pl.program_id(0)
    a, b = slots[number, 0], slots[number, 1]
    kept = row_image.shape[1]
    weigh = kept > rhs

    @pl.when(number == 0)
    def _():
        row_image[...] = jnp.zeros_like(row_image)
        column_image[...] = jnp.zeros_like(column_image)
        dots[...] = jnp.zeros_like(dots)

    @pl.when(slots[number, 2] > 0)
    def _():
        rv, cv = row_values[a, start:start + rhs], column_values[b, start:start + rhs]
        t_high, t_low = high[0], low[0]
        rows, columns = rv, cv
        if weigh:
            ones = jnp.ones((16, rv.shape[1]), jnp.float32)
            rows = jnp.concatenate([rv, ones], axis=0)
            columns = jnp.concatenate([cv, ones], axis=0)
        right_part = times(columns, t_high, t_low, 1)
        left_part = times(rows, t_high, t_low, 0)
        row_image[a] += right_part[:kept]
        column_image[b] += left_part[:kept]
        amount = 2.0 * fold(right_part[:rhs] * rv)
        if weigh:
            amount = amount + fold(right_part[rhs:rhs + 1] * (rv * rv))
            amount = amount + fold(left_part[rhs:rhs + 1] * (cv * cv))
        dots[...] += amount


def turn_kernel(rhs, slots, beta, row_fresh, column_fresh, row_old, column_old, high, low,
                row_image, column_image, dots, row_values, column_values):
    @pl.when(pl.program_id(0) == 0)
    def _():
        factor = beta[:, :1]
        start = row_old.shape[1] - rhs
        for a in range(row_old.shape[0]):
            row_values[a] = row_fresh[a] + factor * row_old[a, start:]
        for b in range(column_old.shape[0]):
            column_values[b] = column_fresh[b] + factor * column_old[b, start:]

    sweep_kernel(rhs, 0, slots, row_values, column_values, high, low,
                 row_image, column_image, dots)


def turn(rhs, slots, beta, row_fresh, column_fresh, row_old, column_old, high, low):
    count, tile = high.shape[0], high.shape[1]
    whole = lambda shape: pl.BlockSpec(shape, lambda i: (0,) * len(shape))
    tiles = pl.BlockSpec((1, tile, tile), lambda i: (i, 0, 0))
    shapes = (row_fresh.shape, column_fresh.shape, (rhs, 128), row_fresh.shape, column_fresh.shape)
    return pl.pallas_call(
        functools.partial(turn_kernel, rhs),
        grid=(count,),
        out_shape=tuple(jax.ShapeDtypeStruct(shape, jnp.float32) for shape in shapes),
        in_specs=[SMEM] + [VMEM] * 5 + [tiles, tiles],
        out_specs=tuple(whole(shape) for shape in shapes),
    )(slots, beta, row_fresh, column_fresh, row_old, column_old, high, low)


def sweep(rhs, start, kept, slots, row_values, column_values, high, low):
    count, tile = high.shape[0], high.shape[1]
    whole = lambda shape: pl.BlockSpec(shape, lambda i: (0,) * len(shape))
    tiles = pl.BlockSpec((1, tile, tile), lambda i: (i, 0, 0))
    shapes = (
        (row_values.shape[0], kept, tile), (column_values.shape[0], kept, tile), (rhs, 128)
    )
    return pl.pallas_call(
        functools.partial(sweep_kernel, rhs, start),
        grid=(count,),
        out_shape=tuple(jax.ShapeDtypeStruct(shape, jnp.float32) for shape in shapes),
        in_specs=[SMEM, VMEM, VMEM, tiles, tiles],
        out_specs=tuple(whole(shape) for shape in shapes),
    )(slots, row_values, column_values, high, low)


def spread(sums):
    return jnp.pad(sums[None, :], ((0, 7), (0, 128 - sums.shape[0])))


def shards(rows, cols, innovations, obs_factors, component, obs_error, coupling, tile_slots):
    slots = tile_slots[0, 0]
    rhs = innovations.shape[0]
    depth = obs_factors.shape[0]
    labels = jnp.pad(component.astype(jnp.float32)[None, :], ((0, 7), (0, 0)))
    packed = jnp.concatenate([obs_factors, labels, innovations], axis=0)
    by_col, by_row, total = gather(
        packed, spread(jnp.sum(innovations * innovations, axis=1)), rows, cols, 0
    )
    norm_now = total[0, :rhs]

    high, low = build(depth, slots, by_col, by_row, coupling)
    row_values, column_values = by_col, by_row

    increment = jnp.zeros_like(innovations)
    residual = innovations
    direction = innovations
    diagonal = None
    for repeat in range(ITERS):
        if repeat == 0:
            row_image, column_image, dots = sweep(
                rhs, depth + 8, rhs + 8, slots, by_col, by_row, high, low
            )
            own = obs_error
        else:
            row_image, column_image, dots, row_values, column_values = turn(
                rhs, slots, jnp.broadcast_to(beta, (rhs, 128)), by_col, by_row,
                row_values, column_values, high, low,
            )
            own = diagonal
        part = jnp.sum(dots, axis=1) + jnp.sum(own[None, :] * direction * direction, axis=1)
        product, total = scatter(row_image, column_image, spread(part), 1 if repeat == 0 else 2)
        if repeat == 0:
            diagonal = obs_error + product[rhs]
        image = diagonal[None, :] * direction + product[:rhs]
        alpha = norm_now / total[0, :rhs]
        increment = increment + alpha[:, None] * direction
        residual = residual - alpha[:, None] * image
        if repeat + 1 < ITERS:
            by_col, by_row, total = gather(
                residual, spread(jnp.sum(residual * residual, axis=1)), rows, cols, 3
            )
            norm_next = total[0, :rhs]
            beta = (norm_next / norm_now)[:, None]
            direction = residual + beta * direction
            norm_now = norm_next
    return (increment, residual)


def solution(mesh):
    return jax.shard_map(
        functools.partial(shards, mesh.shape["row"], mesh.shape["col"]),
        mesh=mesh,
        in_specs=(
            P(None, ("row", "col")),
            P(None, ("row", "col")),
            P(("row", "col")),
            P(("row", "col")),
            P(),
            P("row", "col", None, None),
        ),
        out_specs=(P(None, ("row", "col")), P(None, ("row", "col"))),
        check_vma=False,
    )
```
